256 devices in a mesh: tm: 16 (over z, core), trace: 16 (over y, x).
Axes of the slice: x: 4, y: 4, z: 8, core: 2. Of those that a mesh axis runs over, the one named last changes fastest.
Arguments:
- observed: bfloat16 [256, 8192], P('trace', 'tm'), may hold values from -32 to 32
- sampled: int32 [256, 8192], P('trace', 'tm'), may hold values 0 or 1
- probes: bfloat16 [256, 256, 128], P(None, 'trace'), may hold values from -0.0234375 to 0.0234375
Outputs:
- completed: float32 [256, 8192], P('trace', 'tm')
The draws below stay inside these ranges and needn't reach their ends.
All inputs are finite; a program needn't handle non-finite values. No bound on the sum of `sampled` on one device may be relied on, other than what follows from the above.
Results may differ from the reference program's by a relative error of at most 0.0004.
Values may be sent and summed in bfloat16 or wider, within the bound.
No kernel may reach another device: no remote copies, remote signals or barrier semaphores. Data moves between devices by JAX's collectives and lax.ppermute only.
A program may use at most 64 MiB of HBM per device.

```python
import jax
import jax.numpy as jnp
from jax import lax

TAPS = 256
PROBES = 128
TRACES = 256
SAMPLES = 8192


def draw_observed(key, part):
    keys = jax.random.split(jax.random.fold_in(key, 11), 7)
    count = PROBES
    omega = jax.random.uniform(keys[0], (count,), minval=0.05, maxval=2.5)
    kappa = jax.random.uniform(keys[1], (count,), minval=-1.2, maxval=1.2)
    phase = jax.random.uniform(keys[2], (count,), minval=-3.14159, maxval=3.14159)
    amplitude = jnp.exp(jax.random.uniform(keys[3], (count,), minval=-1.2, maxval=0.4)) * (2.0 / count) ** 0.5
    times = jnp.arange(SAMPLES, dtype=jnp.float32)
    traces = jnp.arange(TRACES, dtype=jnp.float32)

    def add_wave(total, index):
        wave = amplitude[index] * jnp.cos(omega[index] * times[None, :] + kappa[index] * traces[:, None] + phase[index])
        return (total + wave, None)
    signal, unused = lax.scan(add_wave, jnp.zeros((TRACES, SAMPLES), jnp.float32), jnp.arange(count))
    noise = 0.3 * jax.random.normal(keys[4], (TRACES, SAMPLES))
    segment = jnp.exp(jax.random.uniform(keys[5], (SAMPLES // 16,), minval=-0.693, maxval=0.693))
    time_gain = jnp.repeat(segment, 16) * (1.0 + 2.0 * times / SAMPLES)
    trace_gain = jnp.exp(jax.random.uniform(keys[6], (TRACES,), minval=-0.357, maxval=0.336)) * (1.0 + 2.0 * traces / TRACES)
    values = (signal + noise) * time_gain[None, :] * trace_gain[:, None] / 3.0
    return jnp.clip(values, -32.0, 32.0).astype(jnp.bfloat16)


def touch_ends(result, stream_key, low, largest):
    index_at = [jax.random.randint(jax.random.fold_in(stream_key, axis), (), 0, length) for axis, length in enumerate(result.shape)]
    main_axis = result.shape.index(max(result.shape))
    next_to = index_at[:main_axis] + [(index_at[main_axis] + 1) % result.shape[main_axis]] + index_at[main_axis + 1:]
    return result.at[tuple(index_at)].set(low).at[tuple(next_to)].set(largest)


def block_scale(rng, shape, shards, smallest, top_value):
    factor_of = 1.0
    for dim, parts in shards:
        steps = jax.random.uniform(jax.random.fold_in(jax.random.fold_in(rng, 6), dim), (parts,), jnp.float32, smallest / len(shards), top_value / len(shards))
        factor_of = factor_of * jnp.repeat(jnp.exp(steps), shape[dim] // parts).reshape((-1,) + (1,) * (len(shape) - 1 - dim))
    return factor_of


def gaussian(rng, shape, deviation, reach, cuts=(), kind=jnp.bfloat16):
    entries = deviation * jax.random.normal(rng, shape, jnp.float32)
    if cuts:
        entries = entries * block_scale(rng, shape, cuts, -0.22, 0.18)
    return jnp.clip(entries, -reach, reach).astype(kind)


def setup_inputs(seed: int = 0) -> dict:
    streams_of = jax.random.split(jax.random.key(seed), 4)
    return {
        "observed": draw_observed(jax.random.fold_in(streams_of[3], 71), 0),
        "sampled": touch_ends((jax.random.randint(streams_of[1], (TRACES, SAMPLES), 0, 3) < 2).astype(jnp.int32), jax.random.fold_in(streams_of[1], 1), 0, 1),
        "probes": gaussian(streams_of[2], (TAPS, TRACES, PROBES), (TAPS * TRACES) ** -0.5, 0.0234375, ((1, 16),)),
    }


def correlate(signal, kernel, numbers):
    return lax.conv_general_dilated(signal, kernel, (1,), 'VALID', dimension_numbers=numbers, preferred_element_type=jnp.float32)

def reference(observed, sampled, probes):
    taps = probes.shape[0]
    data = jnp.where(sampled == 1, observed, jnp.zeros_like(observed))
    extended = jnp.pad(data, ((0, 0), (0, taps - 1)))
    sketch = correlate(extended[None], probes, ('NCW', 'WIO', 'NWC'))[0]
    gram = jnp.dot(sketch.T.astype(jnp.float32), sketch.astype(jnp.float32), precision=lax.Precision.HIGHEST, preferred_element_type=jnp.float32)
    lower = jnp.linalg.cholesky(gram)
    basis = lax.linalg.triangular_solve(lower, sketch, left_side=False, lower=True, transpose_a=True).astype(jnp.bfloat16)
    coefs = correlate(extended[:, None, :], basis[:, None, :], ('NCW', 'WIO', 'NWC')).astype(jnp.bfloat16)
    kernel = jnp.flip(jnp.transpose(coefs, (1, 2, 0)), 0)
    padded = jnp.pad(basis, ((taps - 1, 0), (0, 0)))
    summed = correlate(padded[None], kernel, ('NWC', 'WIO', 'NCW'))[0]
    counts = jnp.minimum(jnp.arange(SAMPLES, dtype=jnp.int32) + 1, taps).astype(jnp.float32)
    estimate = summed / counts[None, :]
    return jnp.where(sampled == 1, observed.astype(jnp.float32), estimate)
```

```python
import functools

import jax
import jax.numpy as jnp
from jax import lax
from jax.experimental import pallas as pl
from jax.experimental.pallas import tpu as pltpu
from jax.sharding import PartitionSpec as P

F32 = jnp.float32
BF16 = jnp.bfloat16
HI = lax.Precision.HIGHEST
LANES = 128
SUB = 8


def from_behind(block, axis, distance):
    devices = range(lax.axis_size(axis))
    route = [(i - distance, i) for i in devices if i - distance in devices]
    return lax.ppermute(block, axis, route)


def correlate(signal, kernel, numbers):
    return lax.conv_general_dilated(
        signal, kernel, (1,), "VALID", dimension_numbers=numbers, preferred_element_type=jnp.float32
    )


def exchanged(block, axis):
    return lax.all_to_all(block, axis, 0, 0, tiled=True)


def to_all(block, axis):
    copies = lax.axis_size(axis)
    return exchanged(jnp.broadcast_to(block[None], (copies,) + block.shape), axis)


def inverse_of(gram, ranks):
    lane = lax.broadcasted_iota(jnp.int32, (SUB, ranks), 1)
    row = lax.broadcasted_iota(jnp.int32, (SUB, ranks), 0)
    rows = [gram[SUB * i : SUB * i + SUB] for i in range(ranks // SUB)]
    for k in range(ranks // SUB):
        panel = rows[k]
        start = SUB * k
        for s in range(SUB):
            column = panel[:, start + s : start + s + 1]
            pivot = panel[s : s + 1, start + s : start + s + 1]
            scaled = jnp.where(lane[:1] == start + s, 1.0, panel[s : s + 1]) / pivot
            rest = jnp.where(lane == start + s, 0.0, panel) - column * scaled
            panel = jnp.where(row == s, scaled, rest)
        inside = (lane >= start) & (lane < start + SUB)
        for i in range(ranks // SUB):
            if i == k:
                continue
            acc = jnp.where(inside, 0.0, rows[i])
            for s in range(SUB):
                acc = acc - rows[i][:, start + s : start + s + 1] * panel[s : s + 1]
            rows[i] = acc
        rows[k] = panel
    return jnp.concatenate(rows, axis=0)

def kernel(taps, core_ref, own_ref, other_ref, trace_ref, out_ref, s_ref, hankel, sums, sem):
    core = core_ref[0]
    first = pltpu.make_async_copy(own_ref, s_ref.at[core], sem.at[0])
    second = pltpu.make_async_copy(other_ref, s_ref.at[1 - core], sem.at[1])
    first.start(); second.start()
    lane = lax.broadcasted_iota(jnp.int32, (LANES, LANES), 1)
    row = lax.broadcasted_iota(jnp.int32, (LANES, LANES), 0)
    later = lane >= row
    tiles = hankel.shape[0]
    def build(n, _):
        a = jnp.broadcast_to(trace_ref[pl.ds(n, 1), :], (LANES, LANES))
        b = jnp.broadcast_to(trace_ref[pl.ds(n + 1, 1), :], (LANES, LANES))
        t = pltpu.roll(jnp.where(lane + row >= LANES - 1, a, b), 1, 1, stride=1, stride_axis=0)
        hankel[n] = t.astype(BF16)
        return 0
    lax.fori_loop(0, tiles, build, 0)
    first.wait(); second.wait()
    cores, pbs, halves, zs, prow, width = s_ref.shape
    ranks = pbs * prow
    nt = (((1,), (1,)), ((), ()))
    sums[...] = jnp.zeros_like(sums)
    def chunk(z, c, th):
        return s_ref[c, :, th, z].reshape(ranks, width)
    def accumulate(z, _):
        total = None
        for c in range(cores):
            for th in range(halves):
                n = (z * cores + c) * (2 * halves) + 2 * th
                sc = chunk(z, c, th)
                t0, t1, t2 = hankel[n], hankel[n + 1], hankel[n + 2]
                lhs = jnp.concatenate([jnp.concatenate([t0, t1], 1), jnp.concatenate([t1, t2], 1), sc], 0)
                d = lax.dot_general(lhs, sc, nt, preferred_element_type=F32)
                total = d if total is None else total + d
        sums[...] += total
        return 0
    lax.fori_loop(0, zs, accumulate, 0)
    inverse = inverse_of(sums[taps:], ranks)
    weights = jnp.dot(sums[:taps], inverse, precision=HI, preferred_element_type=F32)
    high = weights.astype(BF16)
    low = (weights - high.astype(F32)).astype(BF16)
    pair = jnp.concatenate([high, low], 1)
    flip = jnp.where(lane + row == LANES - 1, 1.0, 0.0).astype(BF16)
    g = jnp.concatenate(
        [jnp.dot(flip, pair[i : i + LANES], preferred_element_type=F32).astype(BF16) for i in range(0, taps, LANES)], 0
    )
    def spread(z, carry):
        behind, rolled = carry
        for c in range(cores):
            for th in range(halves):
                n = (z * cores + c) * (2 * halves) + 2 * th
                sc = chunk(z, c, th)
                y = jnp.dot(g, jnp.concatenate([sc, sc], 0), preferred_element_type=F32)
                for h in range(2):
                    u = y[:LANES, LANES * h : LANES * h + LANES] + behind
                    behind = y[LANES:, LANES * h : LANES * h + LANES]
                    now = pltpu.roll(u, 0, 1, stride=1, stride_axis=0)
                    v = jnp.where(later, now, rolled)
                    rolled = now
                    out_ref[pl.ds(n + h, 1), :] = jnp.sum(v, axis=0, keepdims=True)
        return behind, rolled
    zero = jnp.zeros((LANES, LANES), F32)
    lax.fori_loop(0, zs, spread, (zero, zero))
    t = lax.broadcasted_iota(jnp.int32, out_ref.shape, 0) * LANES + lax.broadcasted_iota(jnp.int32, out_ref.shape, 1)
    out_ref[...] = out_ref[...] / jnp.minimum(t + 1, taps).astype(F32)

def estimate_of(core, own, other, trace, taps):
    groups, zs, prow, width = own.shape
    shape = (groups // 2, 2, zs, prow, width)
    samples = trace.shape[0]
    blocks = samples // LANES
    padded = jnp.pad(trace.astype(F32), (0, 8 * LANES)).reshape(blocks + 8, LANES)
    ranks = groups // 2 * prow
    return pl.pallas_call(
        functools.partial(kernel, taps),
        out_shape=jax.ShapeDtypeStruct((blocks, LANES), F32),
        in_specs=[pl.BlockSpec(memory_space=pltpu.SMEM), pl.BlockSpec(memory_space=pl.ANY), pl.BlockSpec(memory_space=pl.ANY),
                  pl.BlockSpec(memory_space=pltpu.VMEM)],
        out_specs=pl.BlockSpec(memory_space=pltpu.VMEM),
        scratch_shapes=[pltpu.VMEM((2,) + shape, BF16), pltpu.VMEM((blocks + 1, LANES, LANES), BF16),
                        pltpu.VMEM((taps + ranks, ranks), F32), pltpu.SemaphoreType.DMA((2,))],
        name="estimate",
    )(core, own.reshape(shape), other.reshape(shape), padded)


def on_device(observed, sampled, probes):
    taps, traces, ranks = probes.shape
    width = observed.shape[1]
    blocks = lax.axis_size("tm")
    groups = lax.axis_size("trace")
    core = lax.axis_index("tm") % 2
    data = jnp.where(sampled == 1, observed, jnp.zeros_like(observed))
    tail = from_behind(data[:, :taps], "tm", -1)
    extended = jnp.concatenate([data, tail], axis=1)[:, : width + taps - 1]
    partial = correlate(extended[None], probes, ("NCW", "WIO", "NCW"))[0].astype(jnp.bfloat16)
    rows, half = ranks * 2 // groups, width // 2
    parts = partial.reshape(groups // 2, rows, 2, half).transpose(0, 2, 1, 3).reshape(groups, rows, half)
    mine = exchanged(parts, "trace").astype(jnp.float32).sum(0).astype(jnp.bfloat16)
    outgoing = jnp.concatenate(
        [jnp.broadcast_to(mine[None], (blocks, rows, half)), data.reshape(traces, 2, half)], axis=1
    )
    incoming = exchanged(outgoing, "tm")
    trace = incoming[:, rows:].reshape(blocks * width)
    column = incoming[:, :rows].reshape(blocks // 2, 2, rows, half)
    own = to_all(lax.dynamic_index_in_dim(column, core, 1, keepdims=False), "trace").reshape(
        groups, blocks // 2, rows, half
    )
    other = lax.ppermute(own, "tm", [(i, i ^ 1) for i in range(blocks)])
    estimate = estimate_of(core[None].astype(jnp.int32), own, other, trace, taps)
    back = exchanged(estimate.reshape(blocks, width), "tm")
    return jnp.where(sampled == 1, observed.astype(jnp.float32), back)


def solution(mesh):
    in_specs = (P("trace", "tm"), P("trace", "tm"), P(None, "trace", None))
    out_specs = P("trace", "tm")
    return jax.shard_map(
        on_device, mesh=mesh, in_specs=in_specs, out_specs=out_specs, check_vma=False
    )
```

```python
import functools

import jax
import jax.numpy as jnp
from jax import lax
from jax.experimental import pallas as pl
from jax.experimental.pallas import tpu as pltpu
from jax.sharding import PartitionSpec as P

F32 = jnp.float32
BF16 = jnp.bfloat16
HI = lax.Precision.HIGHEST
LANES = 128
SUB = 8
PANEL = 32
STRIPE = 16
LIMIT = 20 << 20


def from_behind(block, axis, distance):
    devices = range(lax.axis_size(axis))
    route = [(i - distance, i) for i in devices if i - distance in devices]
    return lax.ppermute(block, axis, route)


def exchanged(block, axis):
    return lax.all_to_all(block, axis, 0, 0, tiled=True)


def to_all(block, axis):
    copies = lax.axis_size(axis)
    return exchanged(jnp.broadcast_to(block[None], (copies,) + block.shape), axis)


def sketch_kernel(data_ref, tail_ref, probes_ref, out_ref, total):
    traces, width = data_ref.shape
    ranks = probes_ref.shape[1]
    span = STRIPE * traces
    upper = LANES * traces
    total[...] = jnp.zeros_like(total)
    contract = (((0,), (0,)), ((), ()))
    window = jnp.concatenate([data_ref[...], tail_ref[...]], 1).astype(F32)
    length = window.shape[1]

    def stripe(q, window):
        moved = [window if i == 0 else pltpu.roll(window, length - i, 1) for i in range(STRIPE)]
        moved = [x.astype(BF16) for x in moved]
        start = pl.multiple_of(q * span, span)
        for base, first in ((0, 0), (upper, LANES)):
            right = jnp.concatenate([x[:, first : first + width] for x in moved], 0)
            left = probes_ref[pl.ds(base + start, span), :]
            total[...] += lax.dot_general(left, right, contract, preferred_element_type=F32)
        return pltpu.roll(window, length - STRIPE, 1)

    lax.fori_loop(0, LANES // STRIPE, stripe, window)
    groups, tiles, rows, lanes = out_ref.shape
    for g in range(groups):
        for i in range(tiles):
            p, t = g // 2 * rows, (g % 2 * tiles + i) * lanes
            out_ref[g, i] = total[p : p + rows, t : t + lanes].astype(BF16)


def sketch_of(data, tail, probes, groups):
    taps, traces, ranks = probes.shape
    width = data.shape[1]
    return pl.pallas_call(
        sketch_kernel,
        out_shape=jax.ShapeDtypeStruct((groups, width // 2 // LANES, 2 * ranks // groups, LANES), BF16),
        in_specs=[pl.BlockSpec(memory_space=pltpu.VMEM)] * 3,
        out_specs=pl.BlockSpec(memory_space=pltpu.VMEM),
        scratch_shapes=[pltpu.VMEM((ranks, width), F32)],
        name="sketch",
    )(data, tail, probes.reshape(taps * traces, ranks))


def inverse_of(gram, ranks):
    lane = lax.broadcasted_iota(jnp.int32, (SUB, ranks), 1)
    row = lax.broadcasted_iota(jnp.int32, (SUB, ranks), 0)
    everywhere = lambda x: jnp.broadcast_to(x, (SUB, ranks))
    rows = [gram[i : i + SUB] for i in range(0, ranks, SUB)]
    steps = PANEL // SUB
    for top in range(0, ranks, PANEL):
        panel = rows[top // SUB : top // SUB + steps]
        for m in range(steps):
            start = top + SUB * m
            inside = (lane >= start) & (lane < start + SUB)
            columns = [[everywhere(part[:, start + s : start + s + 1]) for s in range(SUB)] for part in panel]
            pivots = columns[m]
            for s in range(SUB):
                picked = [everywhere(column[s : s + 1]) for column in pivots]
                scale = 1.0 / picked[s]
                chosen = row == s
                left = pivots[s]
                for t in range(SUB):
                    if t == s:
                        continue
                    scaled = picked[t] * scale
                    pivots[t] = jnp.where(chosen, scaled, pivots[t] - left * scaled)
                pivots[s] = jnp.where(chosen, scale, -left * scale)
            unit = jnp.where(inside, jnp.where(lane == start + row, 1.0, 0.0), panel[m])
            solved = sum(pivots[s] * everywhere(unit[s : s + 1]) for s in range(SUB))
            spread = [everywhere(solved[s : s + 1]) for s in range(SUB)]
            for r in range(steps):
                if r != m:
                    panel[r] = jnp.where(inside, 0.0, panel[r]) - sum(columns[r][s] * spread[s] for s in range(SUB))
            panel[m] = solved
        done = jnp.concatenate(panel, 0)
        whole = jnp.concatenate(rows, 0)
        wide = lax.broadcasted_iota(jnp.int32, (ranks, ranks), 1)
        within = (wide >= top) & (wide < top + PANEL)
        change = jnp.dot(whole[:, top : top + PANEL], done, precision=HI, preferred_element_type=F32)
        new = jnp.where(within, 0.0, whole) - change
        rows = [new[i : i + SUB] for i in range(0, ranks, SUB)]
        rows[top // SUB : top // SUB + steps] = panel
    return jnp.concatenate(rows, axis=0)


def block_of(ref, *index):
    picked = ref[index[:-2] + (slice(None),) + index[-2:]]
    blocks, tiles, rows, lanes = picked.shape
    return jnp.concatenate([picked[:, i].reshape(blocks * rows, lanes) for i in range(tiles)], 1)


def add_products(first, sketch_ref, hankel_ref, sums_ref, core, taps):
    pbs, halves, zs, tiles = sketch_ref.shape[:4]
    contract = (((1,), (1,)), ((), ()))
    per = halves * tiles

    def accumulate(z, _):
        total = None
        for th in range(halves):
            n = (z * 2 + core) * per + tiles * th
            sc = block_of(sketch_ref, th, z)
            t0, t1, t2 = hankel_ref[n], hankel_ref[n + 1], hankel_ref[n + 2]
            lhs = jnp.concatenate([jnp.concatenate([t0, t1], 1), jnp.concatenate([t1, t2], 1), sc], 0)
            part = lax.dot_general(lhs, sc, contract, preferred_element_type=F32)
            total = part if total is None else total + part
        sums_ref[...] += total
        return 0

    if first:
        sums_ref[...] = jnp.zeros_like(sums_ref)
    lax.fori_loop(0, zs, accumulate, 0, unroll=2)


def prepare_kernel(taps, core_ref, own_ref, trace_ref, hankel_ref, sums_ref):
    lane = lax.broadcasted_iota(jnp.int32, (LANES, LANES), 1)
    row = lax.broadcasted_iota(jnp.int32, (LANES, LANES), 0)
    here = lane + row >= LANES - 1

    def build(n, _):
        a = jnp.broadcast_to(trace_ref[pl.ds(n, 1), :], (LANES, LANES))
        b = jnp.broadcast_to(trace_ref[pl.ds(n + 1, 1), :], (LANES, LANES))
        hankel_ref[n] = pltpu.roll(jnp.where(here, a, b), 1, 1, stride=1, stride_axis=0).astype(BF16)
        return 0

    lax.fori_loop(0, hankel_ref.shape[0], build, 0, unroll=5)
    add_products(True, own_ref, hankel_ref, sums_ref, core_ref[0], taps)


def estimate_kernel(taps, core_ref, own_ref, other_ref, hankel_ref, given_ref, out_ref, s_ref, sums, sem):
    core = core_ref[0]
    first = pltpu.make_async_copy(own_ref, s_ref.at[core], sem.at[0])
    second = pltpu.make_async_copy(other_ref, s_ref.at[1 - core], sem.at[1])
    first.start()
    second.start()
    sums[...] = given_ref[...]
    add_products(False, other_ref, hankel_ref, sums, 1 - core, taps)
    cores, pbs, halves, zs, tiles, prow, lanes = s_ref.shape
    ranks = pbs * prow
    lane = lax.broadcasted_iota(jnp.int32, (LANES, LANES), 1)
    row = lax.broadcasted_iota(jnp.int32, (LANES, LANES), 0)
    later = lane >= row
    inverse = inverse_of(sums[taps:], ranks)
    weights = jnp.dot(sums[:taps], inverse, precision=HI, preferred_element_type=F32)
    high = weights.astype(BF16)
    low = (weights - high.astype(F32)).astype(BF16)
    pair = jnp.concatenate([high, low], 1)
    flip = jnp.where(lane + row == LANES - 1, 1.0, 0.0).astype(BF16)
    g = jnp.concatenate(
        [jnp.dot(flip, pair[i : i + LANES], preferred_element_type=F32).astype(BF16) for i in range(0, taps, LANES)], 0
    )
    first.wait()
    second.wait()

    def spread(z, carry):
        behind, rolled = carry
        for c in range(cores):
            for th in range(halves):
                n = (z * cores + c) * halves * tiles + tiles * th
                sc = block_of(s_ref, c, th, z)
                y = jnp.dot(g, jnp.concatenate([sc, sc], 0), preferred_element_type=F32)
                for h in range(tiles):
                    u = y[:LANES, LANES * h : LANES * h + LANES] + behind
                    behind = y[LANES:, LANES * h : LANES * h + LANES]
                    now = pltpu.roll(u, 0, 1, stride=1, stride_axis=0)
                    v = jnp.where(later, now, rolled)
                    rolled = now
                    out_ref[pl.ds(n + h, 1), :] = jnp.sum(v, axis=0, keepdims=True)
        return behind, rolled

    zero = jnp.zeros((LANES, LANES), F32)
    lax.fori_loop(0, zs, spread, (zero, zero))
    t = lax.broadcasted_iota(jnp.int32, out_ref.shape, 0) * LANES + lax.broadcasted_iota(jnp.int32, out_ref.shape, 1)
    out_ref[...] = out_ref[...] / jnp.minimum(t + 1, taps).astype(F32)


def estimate_of(core, own, other, trace, taps):
    groups, zs, tiles, prow, lanes = own.shape
    shape = (groups // 2, 2, zs, tiles, prow, lanes)
    blocks = trace.shape[0]
    padded = jnp.pad(trace.astype(F32), ((0, SUB), (0, 0)))
    ranks = groups // 2 * prow
    own, other = own.reshape(shape), other.reshape(shape)
    smem, vmem = pl.BlockSpec(memory_space=pltpu.SMEM), pl.BlockSpec(memory_space=pltpu.VMEM)
    flops = blocks * LANES * ranks * (taps + ranks)
    hankel, sums = pl.pallas_call(
        functools.partial(prepare_kernel, taps),
        out_shape=(
            jax.ShapeDtypeStruct((blocks + 1, LANES, LANES), BF16),
            jax.ShapeDtypeStruct((taps + ranks, ranks), F32),
        ),
        in_specs=[smem, vmem, vmem],
        out_specs=(vmem, vmem),
        compiler_params=pltpu.CompilerParams(vmem_limit_bytes=LIMIT),
        cost_estimate=pl.CostEstimate(flops=flops, bytes_accessed=4 << 20, transcendentals=0),
        name="prepare",
    )(core, own, padded)
    return pl.pallas_call(
        functools.partial(estimate_kernel, taps),
        out_shape=jax.ShapeDtypeStruct((blocks, LANES), F32),
        in_specs=[smem, vmem, vmem, vmem, vmem],
        out_specs=vmem,
        scratch_shapes=[
            pltpu.VMEM((2,) + shape, BF16),
            pltpu.VMEM((taps + ranks, ranks), F32),
            pltpu.SemaphoreType.DMA((2,)),
        ],
        compiler_params=pltpu.CompilerParams(vmem_limit_bytes=LIMIT),
        cost_estimate=pl.CostEstimate(flops=4 * flops, bytes_accessed=8 << 20, transcendentals=0),
        name="estimate",
    )(core, own, other, hankel, sums)


def on_device(observed, sampled, probes):
    taps, traces, ranks = probes.shape
    width = observed.shape[1]
    blocks = lax.axis_size("tm")
    groups = lax.axis_size("trace")
    rows, tiles = ranks * 2 // groups, width // 2 // LANES
    lines = width // LANES
    core = (lax.axis_index("tm") & 1).astype(jnp.int32)
    even = core == 0
    data = jnp.where(sampled == 1, observed, jnp.zeros_like(observed))
    tail = from_behind(data[:, :taps], "tm", -1)
    parts = sketch_of(data, tail, probes, groups).reshape(groups, tiles * rows, LANES)
    slots = jnp.pad(data.reshape(traces, lines, LANES), ((0, 0), (0, -lines % SUB), (0, 0)))
    parts, slots, core, even = lax.optimization_barrier((parts, slots, core, even))
    mine = exchanged(parts, "trace").astype(F32).sum(0).astype(BF16)
    outgoing = jnp.concatenate([jnp.broadcast_to(mine[None], (blocks,) + mine.shape), slots], axis=1)
    incoming = exchanged(outgoing, "tm")
    trace = incoming[:, tiles * rows : tiles * rows + lines].reshape(blocks * lines, LANES)
    column = incoming[:, : tiles * rows].reshape(blocks // 2, 2, tiles, rows, LANES)
    kept = jnp.where(even, column[:, 0], column[:, 1])
    own = to_all(kept, "trace").reshape(groups, blocks // 2, tiles, rows, LANES)
    other = lax.ppermute(own, "tm", [(i, i ^ 1) for i in range(blocks)])
    estimate = estimate_of(core[None], own, other, trace, taps)
    back = exchanged(estimate.reshape(blocks, width), "tm")
    return jnp.where(sampled == 1, observed.astype(F32), back)


def solution(mesh):
    in_specs = (P("trace", "tm"), P("trace", "tm"), P(None, "trace", None))
    out_specs = P("trace", "tm")
    return jax.shard_map(
        on_device, mesh=mesh, in_specs=in_specs, out_specs=out_specs, check_vma=False
    )
```

```python
import functools

import jax
import jax.numpy as jnp
from jax import lax
from jax.experimental import pallas as pl
from jax.experimental.pallas import tpu as pltpu
from jax.sharding import PartitionSpec as P

F32 = jnp.float32
BF16 = jnp.bfloat16
HI = lax.Precision.HIGHEST
LANES = 128
SUB = 8
PANEL = 32
LIMIT = 20 << 20
ROWS = 16


def from_behind(block, axis, distance):
    devices = range(lax.axis_size(axis))
    route = [(i - distance, i) for i in devices if i - distance in devices]
    return lax.ppermute(block, axis, route)


def exchanged(block, axis):
    return lax.all_to_all(block, axis, 0, 0, tiled=True)


def to_all(block, axis):
    copies = lax.axis_size(axis)
    return exchanged(jnp.broadcast_to(block[None], (copies,) + block.shape), axis)


def sketch_kernel(half, early_ref, late_ref, probes_ref, *refs):
    even, odd = refs[-2:]
    out_ref = refs[1 if half else 0]
    if not half:
        refs[1][...] = probes_ref[...]
    traces = early_ref.shape[0]
    span = LANES // traces
    step = 2 * LANES
    samples = jnp.concatenate([early_ref[...], late_ref[...]], 1).astype(F32)
    length = samples.shape[1]
    width = early_ref.shape[1]
    moved = [samples if i == 0 else pltpu.roll(samples, length - i, 1) for i in range(span)]
    stacked = jnp.concatenate(moved, 0)
    for i in range(0, length, LANES):
        even[i : i + LANES] = stacked[:, i : i + LANES].T.astype(BF16)
    shifted = pltpu.roll(stacked, length - span, 1)
    for i in range(0, length, LANES):
        odd[i : i + LANES] = shifted[:, i : i + LANES].T.astype(BF16)
    total = None
    for q in range(probes_ref.shape[0] // step):
        first = 2 * span * q
        left = jnp.concatenate([even[first : first + width], odd[first : first + width]], 1)
        part = jnp.dot(left, probes_ref[step * q : step * q + step], preferred_element_type=F32)
        total = part if total is None else total + part
    rows = out_ref.shape[-2]
    for i in range(width // LANES):
        block = total[LANES * i : LANES * i + LANES].T.astype(BF16)
        for p in range(out_ref.shape[0]):
            if half:
                out_ref[p, half, i] = block[rows * p : rows * p + rows]
            else:
                out_ref[p, i] = block[rows * p : rows * p + rows]
    if half:
        out_ref[:, 0] = refs[0][...]


def sketch_of(half, early, late, probes, *given):
    ranks = probes.shape[1]
    length = early.shape[1] + late.shape[1]
    shape = (given[0].shape[:1] + (2,) + given[0].shape[1:]) if given else (ranks // ROWS, early.shape[1] // LANES, ROWS, LANES)
    vmem = pl.BlockSpec(memory_space=pltpu.VMEM)
    return pl.pallas_call(
        functools.partial(sketch_kernel, half),
        out_shape=(jax.ShapeDtypeStruct(shape, BF16),) + (() if half else (jax.ShapeDtypeStruct(probes.shape, BF16),)),
        in_specs=[vmem] * (3 + len(given)),
        out_specs=(vmem,) if half else (vmem, vmem),
        scratch_shapes=[pltpu.VMEM((length, LANES), BF16), pltpu.VMEM((length, LANES), BF16)],
        compiler_params=pltpu.CompilerParams(vmem_limit_bytes=LIMIT),
        cost_estimate=pl.CostEstimate(
            flops=2 * early.shape[1] * probes.size, bytes_accessed=2 * probes.size, transcendentals=0
        ),
        name="sketch",
    )(early, late, probes, *given)


def added(terms):
    while len(terms) > 1:
        terms = [sum(terms[i : i + 2]) for i in range(0, len(terms), 2)]
    return terms[0]


def inverse_of(gram, ranks, beside):
    lane = lax.broadcasted_iota(jnp.int32, (SUB, ranks), 1)
    row = lax.broadcasted_iota(jnp.int32, (SUB, ranks), 0)
    everywhere = lambda x: jnp.broadcast_to(x, (SUB, ranks))
    rows = [gram[i : i + SUB] for i in range(0, ranks, SUB)]
    steps = PANEL // SUB
    for top in range(0, ranks, PANEL):
        panel = rows[top // SUB : top // SUB + steps]
        for m in range(steps):
            start = top + SUB * m
            inside = (lane >= start) & (lane < start + SUB)
            columns = [[everywhere(part[:, start + s : start + s + 1]) for s in range(SUB)] for part in panel]
            pivots = columns[m]
            for s in range(SUB):
                picked = [everywhere(column[s : s + 1]) for column in pivots]
                scale = 1.0 / picked[s]
                chosen = row == s
                left = pivots[s]
                for t in range(SUB):
                    if t == s:
                        continue
                    scaled = picked[t] * scale
                    pivots[t] = jnp.where(chosen, scaled, pivots[t] - left * scaled)
                pivots[s] = jnp.where(chosen, scale, -left * scale)
            unit = jnp.where(inside, jnp.where(lane == start + row, 1.0, 0.0), panel[m])
            solved = added([pivots[s] * everywhere(unit[s : s + 1]) for s in range(SUB)])
            spread = [everywhere(solved[s : s + 1]) for s in range(SUB)]
            for r in range(steps):
                if r != m:
                    panel[r] = jnp.where(inside, 0.0, panel[r]) - added(
                        [columns[r][s] * spread[s] for s in range(SUB)]
                    )
            panel[m] = solved
            beside(start // SUB)
        done = jnp.concatenate(panel, 0)
        whole = jnp.concatenate(rows, 0)
        wide = lax.broadcasted_iota(jnp.int32, (ranks, ranks), 1)
        within = (wide >= top) & (wide < top + PANEL)
        change = jnp.dot(whole[:, top : top + PANEL], done, precision=HI, preferred_element_type=F32)
        new = jnp.where(within, 0.0, whole) - change
        rows = [new[i : i + SUB] for i in range(0, ranks, SUB)]
        rows[top // SUB : top // SUB + steps] = panel
    return jnp.concatenate(rows, axis=0)


def joined(parts):
    return jnp.concatenate([part.reshape(part.shape[0] * part.shape[1], part.shape[2]) for part in parts], 1)


def own_tiles(sketch_ref, r):
    return joined([sketch_ref[:, th, r] for th in range(sketch_ref.shape[1])])


def hankel_tiles(hankel_ref, n, halves):
    top = jnp.concatenate([hankel_ref[n + 2 * th] for th in range(halves)], 1)
    return jnp.concatenate([top, jnp.concatenate([hankel_ref[n + 2 * th + 1] for th in range(halves)], 1)], 0)


def add_products(sketch_ref, hankel_ref, sums_ref, core):
    halves, blocks = sketch_ref.shape[1:3]
    contract = (((1,), (1,)), ((), ()))

    def accumulate(r, _):
        sc = own_tiles(sketch_ref, r)
        lhs = jnp.concatenate([hankel_tiles(hankel_ref, 2 * halves * r + core, halves), sc], 0)
        sums_ref[...] += lax.dot_general(lhs, sc, contract, preferred_element_type=F32)
        return 0

    sums_ref[...] = jnp.zeros_like(sums_ref)
    lax.fori_loop(0, blocks, accumulate, 0, unroll=4)


def prepare_kernel(taps, core_ref, own_ref, trace_ref, hankel_ref, sums_ref):
    lane = lax.broadcasted_iota(jnp.int32, (LANES, LANES), 1)
    row = lax.broadcasted_iota(jnp.int32, (LANES, LANES), 0)
    here = lane + row >= LANES - 1

    def build(n, _):
        a = jnp.broadcast_to(trace_ref[pl.ds(n, 1), :], (LANES, LANES))
        b = jnp.broadcast_to(trace_ref[pl.ds(n + 1, 1), :], (LANES, LANES))
        hankel_ref[n] = pltpu.roll(jnp.where(here, a, b), 1, 1, stride=1, stride_axis=0).astype(BF16)
        return 0

    lax.fori_loop(0, hankel_ref.shape[0], build, 0, unroll=5)
    add_products(own_ref, hankel_ref, sums_ref, core_ref[0])


def estimate_kernel(taps, core_ref, own_ref, other_ref, hankel_ref, given_ref, out_ref, s_ref, sums, sem):
    core = core_ref[0]
    first = pltpu.make_async_copy(own_ref, s_ref.at[core], sem.at[0])
    second = pltpu.make_async_copy(other_ref, s_ref.at[1 - core], sem.at[1])
    first.start()
    second.start()
    sums[...] = given_ref[...]
    tiles, pbs, halves, blocks, prow, lanes = s_ref.shape
    ranks = pbs * prow
    lane = lax.broadcasted_iota(jnp.int32, (LANES, LANES), 1)
    row = lax.broadcasted_iota(jnp.int32, (LANES, LANES), 0)
    later = lane >= row
    contract = (((1,), (1,)), ((), ()))
    grams = []
    for r in range(blocks):
        sc = own_tiles(other_ref, r)
        grams.append(lax.dot_general(sc, sc, contract, preferred_element_type=F32))
    gram = sums[taps:] + added(grams)

    def beside(r):
        lhs = hankel_tiles(hankel_ref, 2 * halves * r + 1 - core, halves)
        sums[:taps] += lax.dot_general(lhs, own_tiles(other_ref, r), contract, preferred_element_type=F32)

    inverse = inverse_of(gram, ranks, beside)
    weights = jnp.dot(sums[:taps], inverse, precision=HI, preferred_element_type=F32)
    high = weights.astype(BF16)
    low = (weights - high.astype(F32)).astype(BF16)
    pair = jnp.concatenate([high, low], 1)
    flip = jnp.where(lane + row == LANES - 1, 1.0, 0.0).astype(BF16)
    g = jnp.concatenate(
        [jnp.dot(flip, pair[i : i + LANES], preferred_element_type=F32).astype(BF16) for i in range(0, taps, LANES)], 0
    )
    first.wait()
    second.wait()

    def spread(r, carry):
        behind, rolled = carry
        for th in range(halves):
            n = (r * halves + th) * tiles
            sc = joined([s_ref[i, :, th, r] for i in range(tiles)])
            y = jnp.dot(g, jnp.concatenate([sc, sc], 0), preferred_element_type=F32)
            for h in range(tiles):
                u = y[:LANES, LANES * h : LANES * h + LANES] + behind
                behind = y[LANES:, LANES * h : LANES * h + LANES]
                now = pltpu.roll(u, 0, 1, stride=1, stride_axis=0)
                v = jnp.where(later, now, rolled)
                rolled = now
                out_ref[pl.ds(n + h, 1), :] = jnp.sum(v, axis=0, keepdims=True)
        return behind, rolled

    zero = jnp.zeros((LANES, LANES), F32)
    lax.fori_loop(0, blocks, spread, (zero, zero), unroll=2)
    t = lax.broadcasted_iota(jnp.int32, out_ref.shape, 0) * LANES + lax.broadcasted_iota(jnp.int32, out_ref.shape, 1)
    out_ref[...] = out_ref[...] / jnp.minimum(t + 1, taps).astype(F32)


def estimate_of(core, own, other, trace, taps):
    groups, _, prow, lanes = own.shape
    shape = (groups // 2, 2) + own.shape[1:]
    blocks = trace.shape[0]
    padded = jnp.pad(trace.astype(F32), ((0, SUB), (0, 0)))
    ranks = groups // 2 * prow
    own, other = own.reshape(shape), other.reshape(shape)
    smem, vmem = pl.BlockSpec(memory_space=pltpu.SMEM), pl.BlockSpec(memory_space=pltpu.VMEM)
    flops = blocks * LANES * ranks * (taps + ranks)
    hankel, sums = pl.pallas_call(
        functools.partial(prepare_kernel, taps),
        out_shape=(
            jax.ShapeDtypeStruct((blocks + 1, LANES, LANES), BF16),
            jax.ShapeDtypeStruct((taps + ranks, ranks), F32),
        ),
        in_specs=[smem, vmem, vmem],
        out_specs=(vmem, vmem),
        compiler_params=pltpu.CompilerParams(vmem_limit_bytes=LIMIT),
        cost_estimate=pl.CostEstimate(flops=flops, bytes_accessed=4 << 20, transcendentals=0),
        name="prepare",
    )(core, own, padded)
    return pl.pallas_call(
        functools.partial(estimate_kernel, taps),
        out_shape=jax.ShapeDtypeStruct((blocks, LANES), F32),
        in_specs=[smem, vmem, vmem, vmem, vmem],
        out_specs=vmem,
        scratch_shapes=[
            pltpu.VMEM((2,) + shape, BF16),
            pltpu.VMEM((taps + ranks, ranks), F32),
            pltpu.SemaphoreType.DMA((2,)),
        ],
        compiler_params=pltpu.CompilerParams(vmem_limit_bytes=LIMIT),
        cost_estimate=pl.CostEstimate(flops=4 * flops, bytes_accessed=8 << 20, transcendentals=0),
        name="estimate",
    )(core, own, other, hankel, sums)


def on_device(observed, sampled, probes):
    taps, traces, ranks = probes.shape
    width = observed.shape[1]
    blocks = lax.axis_size("tm")
    groups = lax.axis_size("trace")
    rows, tiles = ranks * 2 // groups, width // 2 // LANES
    lines = width // LANES
    core = (lax.axis_index("tm") & 1).astype(jnp.int32)
    data = jnp.where(sampled == 1, observed, jnp.zeros_like(observed))
    middle = width // 2
    tail = from_behind(data[:, :middle], "tm", -1)
    slots = jnp.pad(data.reshape(traces, lines, LANES), ((0, 0), (0, -lines % SUB), (0, 0)))
    flat = probes.reshape(taps * traces, ranks)
    early, late = data[:, :middle], data[:, middle:]
    parts, flat = sketch_of(0, early, late, flat)
    (parts,) = sketch_of(1, late, tail, flat, parts)
    parts = parts.reshape(groups, tiles * rows, LANES)
    parts, slots, core = lax.optimization_barrier((parts, slots, core))
    mine = exchanged(parts, "trace").astype(F32).sum(0).astype(BF16).reshape(tiles, rows, LANES)
    lots = jnp.broadcast_to(mine[None], (blocks // tiles,) + mine.shape).reshape(blocks, rows, LANES)
    incoming = exchanged(jnp.concatenate([lots, slots], axis=1), "tm")
    trace = incoming[:, rows : rows + lines].reshape(blocks * lines, LANES)
    own = to_all(incoming[:, :rows], "trace").reshape(groups, blocks, rows, LANES)
    other = lax.ppermute(own, "tm", [(i, i ^ 1) for i in range(blocks)])
    estimate = estimate_of(core[None], own, other, trace, taps)
    back = exchanged(estimate.reshape(blocks, width), "tm")
    return jnp.where(sampled == 1, observed.astype(F32), back)


def solution(mesh):
    in_specs = (P("trace", "tm"), P("trace", "tm"), P(None, "trace", None))
    out_specs = P("trace", "tm")
    return jax.shard_map(
        on_device, mesh=mesh, in_specs=in_specs, out_specs=out_specs, check_vma=False
    )
```

```python
import functools

import jax
import jax.numpy as jnp
from jax import lax
from jax.experimental import pallas as pl
from jax.experimental.pallas import tpu as pltpu
from jax.sharding import PartitionSpec as P

F32 = jnp.float32
BF16 = jnp.bfloat16
HI = lax.Precision.HIGHEST
LANES = 128
SUB = 8
PANEL = 32
LIMIT = 20 << 20
ROWS = 16


def from_behind(block, axis, distance):
    devices = range(lax.axis_size(axis))
    route = [(i - distance, i) for i in devices if i - distance in devices]
    return lax.ppermute(block, axis, route)


def exchanged(block, axis):
    return lax.all_to_all(block, axis, 0, 0, tiled=True)


def to_all(block, axis):
    copies = lax.axis_size(axis)
    return exchanged(jnp.broadcast_to(block[None], (copies,) + block.shape), axis)


def sketch_kernel(half, early_ref, late_ref, probes_ref, *refs):
    even, odd = refs[-2:]
    out_ref = refs[1 if half else 0]
    if not half:
        refs[1][...] = probes_ref[...]
    traces = early_ref.shape[0]
    span = LANES // traces
    step = 2 * LANES
    samples = jnp.concatenate([early_ref[...], late_ref[...]], 1).astype(F32)
    length = samples.shape[1]
    width = early_ref.shape[1]
    moved = [samples if i == 0 else pltpu.roll(samples, length - i, 1) for i in range(span)]
    stacked = jnp.concatenate(moved, 0)
    for i in range(0, length, LANES):
        even[i : i + LANES] = stacked[:, i : i + LANES].T.astype(BF16)
    shifted = pltpu.roll(stacked, length - span, 1)
    for i in range(0, length, LANES):
        odd[i : i + LANES] = shifted[:, i : i + LANES].T.astype(BF16)
    total = None
    for q in range(probes_ref.shape[0] // step):
        first = 2 * span * q
        left = jnp.concatenate([even[first : first + width], odd[first : first + width]], 1)
        part = jnp.dot(left, probes_ref[step * q : step * q + step], preferred_element_type=F32)
        total = part if total is None else total + part
    rows = out_ref.shape[-2]
    for i in range(width // LANES):
        block = total[LANES * i : LANES * i + LANES].T.astype(BF16)
        for p in range(out_ref.shape[0]):
            if half:
                out_ref[p, half, i] = block[rows * p : rows * p + rows]
            else:
                out_ref[p, i] = block[rows * p : rows * p + rows]
    if half:
        out_ref[:, 0] = refs[0][...]


def sketch_of(half, early, late, probes, *given):
    ranks = probes.shape[1]
    length = early.shape[1] + late.shape[1]
    shape = (given[0].shape[:1] + (2,) + given[0].shape[1:]) if given else (ranks // ROWS, early.shape[1] // LANES, ROWS, LANES)
    vmem = pl.BlockSpec(memory_space=pltpu.VMEM)
    return pl.pallas_call(
        functools.partial(sketch_kernel, half),
        out_shape=(jax.ShapeDtypeStruct(shape, BF16),) + (() if half else (jax.ShapeDtypeStruct(probes.shape, BF16),)),
        in_specs=[vmem] * (3 + len(given)),
        out_specs=(vmem,) if half else (vmem, vmem),
        scratch_shapes=[pltpu.VMEM((length, LANES), BF16), pltpu.VMEM((length, LANES), BF16)],
        compiler_params=pltpu.CompilerParams(vmem_limit_bytes=LIMIT),
        cost_estimate=pl.CostEstimate(
            flops=2 * early.shape[1] * probes.size, bytes_accessed=2 * probes.size, transcendentals=0
        ),
        name="sketch",
    )(early, late, probes, *given)


def added(terms):
    while len(terms) > 1:
        terms = [sum(terms[i : i + 2]) for i in range(0, len(terms), 2)]
    return terms[0]


def inverse_of(gram, ranks, beside):
    lane = lax.broadcasted_iota(jnp.int32, (SUB, ranks), 1)
    row = lax.broadcasted_iota(jnp.int32, (SUB, ranks), 0)
    everywhere = lambda x: jnp.broadcast_to(x, (SUB, ranks))
    rows = [gram[i : i + SUB] for i in range(0, ranks, SUB)]
    steps = PANEL // SUB
    for top in range(0, ranks, PANEL):
        panel = rows[top // SUB : top // SUB + steps]
        for m in range(steps):
            start = top + SUB * m
            inside = (lane >= start) & (lane < start + SUB)
            columns = [[everywhere(part[:, start + s : start + s + 1]) for s in range(SUB)] for part in panel]
            pivots = columns[m]
            for s in range(SUB):
                picked = [everywhere(column[s : s + 1]) for column in pivots]
                scale = 1.0 / picked[s]
                chosen = row == s
                left = pivots[s]
                for t in range(SUB):
                    if t == s:
                        continue
                    scaled = picked[t] * scale
                    pivots[t] = jnp.where(chosen, scaled, pivots[t] - left * scaled)
                pivots[s] = jnp.where(chosen, scale, -left * scale)
            unit = jnp.where(inside, jnp.where(lane == start + row, 1.0, 0.0), panel[m])
            solved = added([pivots[s] * everywhere(unit[s : s + 1]) for s in range(SUB)])
            spread = [everywhere(solved[s : s + 1]) for s in range(SUB)]
            for r in range(steps):
                if r != m:
                    panel[r] = jnp.where(inside, 0.0, panel[r]) - added(
                        [columns[r][s] * spread[s] for s in range(SUB)]
                    )
            panel[m] = solved
            beside(start // SUB)
        done = jnp.concatenate(panel, 0)
        whole = jnp.concatenate(rows, 0)
        wide = lax.broadcasted_iota(jnp.int32, (ranks, ranks), 1)
        within = (wide >= top) & (wide < top + PANEL)
        change = jnp.dot(whole[:, top : top + PANEL], done, precision=HI, preferred_element_type=F32)
        new = jnp.where(within, 0.0, whole) - change
        rows = [new[i : i + SUB] for i in range(0, ranks, SUB)]
        rows[top // SUB : top // SUB + steps] = panel
    return jnp.concatenate(rows, axis=0)


def joined(parts):
    return jnp.concatenate([part.reshape(part.shape[0] * part.shape[1], part.shape[2]) for part in parts], 1)


def own_tiles(sketch_ref, r):
    return joined([sketch_ref[:, th, r] for th in range(sketch_ref.shape[1])])


def hankel_tiles(hankel_ref, n, halves):
    top = jnp.concatenate([hankel_ref[n + 2 * th] for th in range(halves)], 1)
    return jnp.concatenate([top, jnp.concatenate([hankel_ref[n + 2 * th + 1] for th in range(halves)], 1)], 0)


def add_products(sketch_ref, hankel_ref, sums_ref, core):
    halves, blocks = sketch_ref.shape[1:3]
    contract = (((1,), (1,)), ((), ()))

    def accumulate(r, _):
        sc = own_tiles(sketch_ref, r)
        lhs = jnp.concatenate([hankel_tiles(hankel_ref, 2 * halves * r + core, halves), sc], 0)
        sums_ref[...] += lax.dot_general(lhs, sc, contract, preferred_element_type=F32)
        return 0

    sums_ref[...] = jnp.zeros_like(sums_ref)
    lax.fori_loop(0, blocks, accumulate, 0, unroll=8)


def prepare_kernel(taps, core_ref, own_ref, trace_ref, hankel_ref, sums_ref):
    lane = lax.broadcasted_iota(jnp.int32, (LANES, LANES), 1)
    row = lax.broadcasted_iota(jnp.int32, (LANES, LANES), 0)
    here = lane + row >= LANES - 1

    def build(n, _):
        a = jnp.broadcast_to(trace_ref[pl.ds(n, 1), :], (LANES, LANES))
        b = jnp.broadcast_to(trace_ref[pl.ds(n + 1, 1), :], (LANES, LANES))
        hankel_ref[n] = pltpu.roll(jnp.where(here, a, b), 1, 1, stride=1, stride_axis=0).astype(BF16)
        return 0

    lax.fori_loop(0, hankel_ref.shape[0], build, 0, unroll=13)
    add_products(own_ref, hankel_ref, sums_ref, core_ref[0])


def estimate_kernel(taps, core_ref, own_ref, other_ref, hankel_ref, given_ref, out_ref, s_ref, sums, sem):
    core = core_ref[0]
    first = pltpu.make_async_copy(own_ref, s_ref.at[core], sem.at[0])
    second = pltpu.make_async_copy(other_ref, s_ref.at[1 - core], sem.at[1])
    first.start()
    second.start()
    sums[...] = given_ref[...]
    tiles, pbs, halves, blocks, prow, lanes = s_ref.shape
    ranks = pbs * prow
    lane = lax.broadcasted_iota(jnp.int32, (LANES, LANES), 1)
    row = lax.broadcasted_iota(jnp.int32, (LANES, LANES), 0)
    later = lane >= row
    contract = (((1,), (1,)), ((), ()))
    whole = jnp.concatenate([own_tiles(other_ref, r) for r in range(blocks)], 1)
    gram = sums[taps:] + lax.dot_general(whole, whole, contract, preferred_element_type=F32)

    def beside(r):
        lhs = hankel_tiles(hankel_ref, 2 * halves * r + 1 - core, halves)
        sums[:taps] += lax.dot_general(lhs, own_tiles(other_ref, r), contract, preferred_element_type=F32)

    inverse = inverse_of(gram, ranks, beside)
    weights = jnp.dot(sums[:taps], inverse, precision=HI, preferred_element_type=F32)
    high = weights.astype(BF16)
    low = (weights - high.astype(F32)).astype(BF16)
    pair = jnp.concatenate([high, low], 1)
    flip = jnp.where(lane + row == LANES - 1, 1.0, 0.0).astype(BF16)
    g = jnp.concatenate(
        [jnp.dot(flip, pair[i : i + LANES], preferred_element_type=F32).astype(BF16) for i in range(0, taps, LANES)], 0
    )
    first.wait()
    second.wait()

    def spread(r, carry):
        behind, rolled = carry
        for th in range(halves):
            n = (r * halves + th) * tiles
            sc = joined([s_ref[i, :, th, r] for i in range(tiles)])
            y = jnp.dot(g, jnp.concatenate([sc, sc], 0), preferred_element_type=F32)
            for h in range(tiles):
                u = y[:LANES, LANES * h : LANES * h + LANES] + behind
                behind = y[LANES:, LANES * h : LANES * h + LANES]
                now = pltpu.roll(u, 0, 1, stride=1, stride_axis=0)
                v = jnp.where(later, now, rolled)
                rolled = now
                out_ref[pl.ds(n + h, 1), :] = jnp.sum(v, axis=0, keepdims=True)
        return behind, rolled

    zero = jnp.zeros((LANES, LANES), F32)
    lax.fori_loop(0, blocks, spread, (zero, zero), unroll=2)
    t = lax.broadcasted_iota(jnp.int32, out_ref.shape, 0) * LANES + lax.broadcasted_iota(jnp.int32, out_ref.shape, 1)
    out_ref[...] = out_ref[...] / jnp.minimum(t + 1, taps).astype(F32)


def estimate_of(core, own, other, trace, taps):
    groups, _, prow, lanes = own.shape
    shape = (groups // 2, 2) + own.shape[1:]
    blocks = trace.shape[0]
    padded = jnp.pad(trace.astype(F32), ((0, SUB), (0, 0)))
    ranks = groups // 2 * prow
    own, other = own.reshape(shape), other.reshape(shape)
    smem, vmem = pl.BlockSpec(memory_space=pltpu.SMEM), pl.BlockSpec(memory_space=pltpu.VMEM)
    flops = blocks * LANES * ranks * (taps + ranks)
    hankel, sums = pl.pallas_call(
        functools.partial(prepare_kernel, taps),
        out_shape=(
            jax.ShapeDtypeStruct((blocks + 1, LANES, LANES), BF16),
            jax.ShapeDtypeStruct((taps + ranks, ranks), F32),
        ),
        in_specs=[smem, vmem, vmem],
        out_specs=(vmem, vmem),
        compiler_params=pltpu.CompilerParams(vmem_limit_bytes=LIMIT),
        cost_estimate=pl.CostEstimate(flops=flops, bytes_accessed=4 << 20, transcendentals=0),
        name="prepare",
    )(core, own, padded)
    return pl.pallas_call(
        functools.partial(estimate_kernel, taps),
        out_shape=jax.ShapeDtypeStruct((blocks, LANES), F32),
        in_specs=[smem, vmem, vmem, vmem, vmem],
        out_specs=vmem,
        scratch_shapes=[
            pltpu.VMEM((2,) + shape, BF16),
            pltpu.VMEM((taps + ranks, ranks), F32),
            pltpu.SemaphoreType.DMA((2,)),
        ],
        compiler_params=pltpu.CompilerParams(vmem_limit_bytes=LIMIT),
        cost_estimate=pl.CostEstimate(flops=4 * flops, bytes_accessed=8 << 20, transcendentals=0),
        name="estimate",
    )(core, own, other, hankel, sums)


def on_device(observed, sampled, probes):
    taps, traces, ranks = probes.shape
    width = observed.shape[1]
    blocks = lax.axis_size("tm")
    groups = lax.axis_size("trace")
    rows, tiles = ranks * 2 // groups, width // 2 // LANES
    lines = width // LANES
    core = (lax.axis_index("tm") & 1).astype(jnp.int32)
    data = jnp.where(sampled == 1, observed, jnp.zeros_like(observed))
    middle = width // 2
    tail = from_behind(data[:, :middle], "tm", -1)
    slots = jnp.pad(data.reshape(traces, lines, LANES), ((0, 0), (0, -lines % SUB), (0, 0)))
    flat = probes.reshape(taps * traces, ranks)
    early, late = data[:, :middle], data[:, middle:]
    parts, flat = sketch_of(0, early, late, flat)
    (parts,) = sketch_of(1, late, tail, flat, parts)
    parts = parts.reshape(groups, tiles * rows, LANES)
    parts, slots, core = lax.optimization_barrier((parts, slots, core))
    mine = exchanged(parts, "trace").astype(F32).sum(0).astype(BF16).reshape(tiles, rows, LANES)
    lots = jnp.broadcast_to(mine[None], (blocks // tiles,) + mine.shape).reshape(blocks, rows, LANES)
    incoming = exchanged(jnp.concatenate([lots, slots], axis=1), "tm")
    trace = incoming[:, rows : rows + lines].reshape(blocks * lines, LANES)
    own = to_all(incoming[:, :rows], "trace").reshape(groups, blocks, rows, LANES)
    other = lax.ppermute(own, "tm", [(i, i ^ 1) for i in range(blocks)])
    estimate = estimate_of(core[None], own, other, trace, taps)
    back = exchanged(estimate.reshape(blocks, width), "tm")
    return jnp.where(sampled == 1, observed.astype(F32), back)


def solution(mesh):
    in_specs = (P("trace", "tm"), P("trace", "tm"), P(None, "trace", None))
    out_specs = P("trace", "tm")
    return jax.shard_map(
        on_device, mesh=mesh, in_specs=in_specs, out_specs=out_specs, check_vma=False
    )
```
